32 devices in a mesh: chan: 2 (over x), row: 4 (over z), col: 4 (over y, core).
Axes of the slice: x: 2, y: 2, z: 4, core: 2. Of those that a mesh axis runs over, the one named last changes fastest.
Arguments:
- amplitudes: bfloat16 [2, 3584, 512], P('chan', 'row', 'col'), may hold values from -6 to 6
- ladder_block: bfloat16 [2, 3584, 3584], P('chan', 'col', 'row'), may hold values from -0.09375 to 0.09375
- cycle_block: bfloat16 [2, 3584, 3584], P('chan', 'col', 'row'), may hold values from -0.09375 to 0.09375
- recoupling: float32 [2, 2], P(None, 'chan'), may hold values from -1.5 to 1.5
- row_order: int32 [2, 3584], P('chan'), may hold values from 0 to 3583, as said below
- live_rows: int32 [2], P('chan'), may hold values from 1792 to 3584, as said below
Outputs:
- update: bfloat16 [2, 3584, 512], P('chan', 'col', 'row')
The draws below stay inside these ranges and needn't reach their ends.
Inputs may be any that keep to these rules, and one draw needn't show every extreme that they name: Within each aligned block of 896 entries of a channel's row, row_order is a permutation of that block's own indices. `live_rows`: some channel is fully occupied and some channel holds exactly 1792 states in every draw.
All inputs are finite; a program needn't handle non-finite values.
Results may differ from the reference program's by a relative error of at most 0.0034.
Values may be sent and summed in bfloat16 or wider, within the bound.
No kernel may reach another device: no remote copies, remote signals or barrier semaphores. Data moves between devices by JAX's collectives and lax.ppermute only.
A program may use at most 64 MiB of HBM per device.

```python
import jax
import jax.numpy as jnp
from jax import lax

PP = 3584
HH = 512
CHANNELS = 2
BLOCK = 896
GROUP = 448


def shuffle_block(subkey):
    return jax.random.permutation(subkey, BLOCK)


def draw_row_order(key, part):
    block_count = PP // BLOCK
    subkeys = jax.random.split(jax.random.fold_in(key, 3), CHANNELS * block_count)
    shuffled = jax.vmap(shuffle_block)(subkeys)
    offsets = jnp.arange(CHANNELS * block_count, dtype=jnp.int32) % block_count * BLOCK
    return (shuffled.astype(jnp.int32) + offsets[:, None]).reshape(CHANNELS, PP).astype(jnp.int32)


def draw_live_rows(key, part):
    counts = jax.random.randint(jax.random.fold_in(key, 1), (CHANNELS,), PP // 2, PP + 1)
    picks = jax.random.permutation(jax.random.fold_in(key, 2), CHANNELS)
    counts = counts.at[picks[0]].set(PP).at[picks[1]].set(PP // 2)
    return counts.astype(jnp.int32)


def block_levels(own_key, shape, cuts, least, largest):
    gain = 1.0
    for dim, parts in cuts:
        steps = jax.random.uniform(jax.random.fold_in(jax.random.fold_in(own_key, 6), dim), (parts,), jnp.float32, least / len(cuts), largest / len(cuts))
        gain = gain * jnp.repeat(jnp.exp(steps), shape[dim] // parts).reshape((-1,) + (1,) * (len(shape) - 1 - dim))
    return gain


def gaussian(own_key, extent, width, limit, cuts=(), kind=jnp.bfloat16):
    values = jax.random.normal(own_key, extent, jnp.float32) * width
    if len(cuts) > 0:
        values = block_levels(own_key, extent, cuts, -0.22, 0.18) * values
    return jnp.clip(values, min=-limit, max=limit).astype(kind)


def setup_inputs(seed: int = 0) -> dict:
    splits = jax.random.split(jax.random.key(seed), 7)
    return {
        "amplitudes": gaussian(splits[0], (CHANNELS, PP, HH), 1.0, 6.0, ((0, 2), (1, 4), (2, 4))),
        "ladder_block": gaussian(splits[1], (CHANNELS, PP, PP), PP ** -0.5, 0.09375, ((0, 2), (1, 4), (2, 4))),
        "cycle_block": gaussian(splits[2], (CHANNELS, PP, PP), PP ** -0.5, 0.09375, ((0, 2), (1, 4), (2, 4))),
        "recoupling": jnp.clip(jax.random.uniform(splits[3], (CHANNELS, CHANNELS), jnp.float32, -1.5, 1.5) * block_levels(splits[3], (CHANNELS, CHANNELS), ((1, 2),), -0.4, 0.0), -1.5, 1.5),
        "row_order": draw_row_order(jax.random.fold_in(splits[6], 71), 0),
        "live_rows": draw_live_rows(jax.random.fold_in(splits[6], 71), 0),
    }


def product(operands):
    return jnp.dot(operands[0], operands[1], preferred_element_type=jnp.float32)


def place_rows(values, order):
    return jnp.zeros_like(values).at[order].set(values)


def reference(amplitudes, ladder_block, cycle_block, recoupling, row_order, live_rows):
    row_index = jnp.arange(PP, dtype=jnp.int32)
    living = row_index[None, :] < live_rows[:, None]
    masked = jnp.where(living[:, :, None], amplitudes, jnp.zeros((), jnp.bfloat16))
    ladder = lax.map(product, (ladder_block, masked))
    block_count = PP // BLOCK
    permuted = jnp.take_along_axis(masked, row_order[:, :, None], axis=1)
    grouped = permuted.astype(jnp.float32).reshape(CHANNELS, block_count, CHANNELS, GROUP, HH)
    weighted = grouped * recoupling[:, None, :, None, None]
    crossed = jnp.transpose(weighted, (2, 1, 0, 3, 4)).reshape(CHANNELS, PP, HH).astype(jnp.bfloat16)
    cycle_part = lax.map(product, (cycle_block, crossed))
    returning = cycle_part.reshape(CHANNELS, block_count, CHANNELS, GROUP, HH)
    returning = jnp.transpose(returning, (2, 1, 0, 3, 4)) * recoupling[:, None, :, None, None]
    returning = returning.reshape(CHANNELS, PP, HH)
    cycle_term = jax.vmap(place_rows)(returning, row_order)
    summed = ladder + cycle_term
    return jnp.where(living[:, :, None], summed, jnp.float32(0.0)).astype(jnp.bfloat16)
```

```python
import jax
import jax.numpy as jnp
from jax import lax
from jax.sharding import PartitionSpec as P


def place_rows(values, order):
    return jnp.zeros_like(values).at[order].set(values)


def multiply(matrix, operand):
    return jnp.einsum("jpq,jqh->jph", matrix, operand, preferred_element_type=jnp.float32)


def general_shards(amplitudes, ladder_block, cycle_block, recoupling, row_order, live_rows):
    owned, block_rows, local_cols = amplitudes.shape
    chan_size = lax.axis_size("chan")
    channels = chan_size * owned
    groups = block_rows // channels
    row_place = lax.axis_index("row")
    col_place = lax.axis_index("col")
    row_index = jnp.arange(block_rows, dtype=jnp.int32)
    living_in = (row_place * block_rows + row_index)[None, :] < live_rows[:, None]
    masked = jnp.where(living_in[:, :, None], amplitudes, jnp.zeros((), jnp.bfloat16))
    order_in = (
        lax.dynamic_slice_in_dim(row_order, row_place * block_rows, block_rows, 1)
        - row_place * block_rows
    )
    order_out = (
        lax.dynamic_slice_in_dim(row_order, col_place * block_rows, block_rows, 1)
        - col_place * block_rows
    )
    coupling = jnp.transpose(recoupling)
    ladder = multiply(ladder_block, lax.all_gather(masked, "col", axis=2, tiled=True))
    permuted = jnp.take_along_axis(masked, order_in[:, :, None], axis=1)
    arrived = lax.all_to_all(
        permuted.reshape(owned, chan_size, owned, groups, masked.shape[2]),
        "chan",
        split_axis=1,
        concat_axis=1,
        tiled=True,
    )
    columns = arrived.shape[4]
    arranged = jnp.transpose(arrived, (2, 1, 0, 3, 4)).reshape(owned, channels, groups, columns)
    scaled = arranged.astype(jnp.float32) * coupling[:, :, None, None]
    crossed_local = scaled.astype(jnp.bfloat16).reshape(owned, block_rows, columns)
    cycle_part = multiply(cycle_block, lax.all_gather(crossed_local, "col", axis=2, tiled=True))
    columns = cycle_part.shape[2]
    scaled = cycle_part.reshape(owned, channels, groups, columns) * coupling[:, :, None, None]
    returned = lax.all_to_all(
        scaled.reshape(owned, chan_size, owned, groups, columns),
        "chan",
        split_axis=1,
        concat_axis=1,
        tiled=True,
    )
    columns = returned.shape[4]
    arranged = jnp.transpose(returned, (2, 1, 0, 3, 4)).reshape(owned, block_rows, columns)
    cycle_term = jax.vmap(place_rows)(arranged, order_out)
    summed = lax.psum_scatter(ladder + cycle_term, "row", scatter_dimension=2, tiled=True)
    living_out = (col_place * block_rows + row_index)[None, :] < live_rows[:, None]
    return jnp.where(living_out[:, :, None], summed, jnp.float32(0.0)).astype(jnp.bfloat16)


def swap(values, axis, bit):
    size = lax.axis_size(axis)
    return lax.ppermute(values, axis, [(i, i ^ bit) for i in range(size)])


def cross_swap(values, bit):
    cols = lax.axis_size("col")
    pairs = []
    for chan in range(2):
        for col in range(cols):
            pairs.append((chan * cols + col, (1 - chan) * cols + (col ^ bit)))
    return lax.ppermute(values, ("chan", "col"), pairs)


def dot(left, right):
    return jnp.dot(left, right, preferred_element_type=jnp.float32)


def pair_shards(amplitudes, ladder_block, cycle_block, recoupling, row_order, live_rows):
    own = amplitudes[0]
    block_rows, width = own.shape
    group = block_rows // 2
    bf16 = jnp.bfloat16
    chan = lax.axis_index("chan")
    row = lax.axis_index("row")
    col = lax.axis_index("col")
    live = live_rows[0]
    states = jnp.arange(block_rows, dtype=jnp.int32)
    live_in = states + row * block_rows < live
    live_out = states + col * block_rows < live
    order_in = lax.dynamic_slice_in_dim(row_order[0], row * block_rows, block_rows)
    order_in = (order_in - row * block_rows).reshape(2, group)
    order_out = lax.dynamic_slice_in_dim(row_order[0], col * block_rows, block_rows)
    order_out = (order_out - col * block_rows).reshape(2, group)

    def pick(pair, other):
        first = (chan == 0) != other
        return jnp.where(first, pair[0], pair[1])

    weight_own = pick(recoupling[:, 0], False)
    weight_other = pick(recoupling[:, 0], True)

    def one_hot_in(order):
        return ((order[:, None] == states[None, :]) & live_in[None, :]).astype(bf16)

    sent = dot(one_hot_in(pick(order_in, True)), own).astype(bf16)

    own_y = swap(own, "col", 2)
    got = swap(sent, "chan", 1)
    got_y = cross_swap(sent, 2)
    own_core = swap(own, "col", 1)
    own_ycore = swap(own_y, "col", 1)
    got_core = swap(got, "col", 1)
    got_ycore = swap(got_y, "col", 1)
    gathered = jnp.concatenate([own, own_core, own_y, own_ycore], axis=1)
    arrived = jnp.concatenate([got, got_core, got_y, got_ycore], axis=1)

    order_cat = jnp.concatenate([pick(order_out, False), pick(order_out, True)])
    turn = (order_cat[:, None] == states[None, :]).astype(bf16)
    ladder_rows = dot(turn, ladder_block[0])
    ladder_rows = jnp.where(live_in[None, :], ladder_rows, 0.0).astype(bf16)
    ladder = dot(ladder_rows, gathered)

    kept = dot(one_hot_in(pick(order_in, False)), gathered)
    kept = (kept * weight_own).astype(bf16)
    arrived = (arrived.astype(jnp.float32) * weight_other).astype(bf16)
    first = chan == 0
    crossed = jnp.concatenate(
        [jnp.where(first, kept, arrived), jnp.where(first, arrived, kept)], axis=0
    )
    cycle_own = lax.dynamic_slice_in_dim(cycle_block[0], chan * group, group)
    cycle_other = lax.dynamic_slice_in_dim(cycle_block[0], (1 - chan) * group, group)
    leaving = (dot(cycle_other, crossed) * weight_other).astype(bf16)
    staying = dot(cycle_own, crossed) * weight_own

    sum_own = ladder[:group] + staying
    start = jnp.bitwise_xor(row, col)

    def slab(values, step):
        place = jnp.bitwise_xor(start, step)
        return lax.dynamic_slice_in_dim(values, place * width, width, 1)

    returned = [swap(slab(leaving, step), "chan", 1) for step in range(4)]

    total_own = slab(sum_own, 0)
    for step in (1, 2, 3):
        total_own += swap(slab(sum_own, step).astype(bf16), "row", step).astype(jnp.float32)
    ladder_other = ladder[group:]
    total_other = slab(ladder_other, 0) + returned[0].astype(jnp.float32)
    for step in (1, 2, 3):
        part = slab(ladder_other, step) + returned[step].astype(jnp.float32)
        total_other += swap(part.astype(bf16), "row", step).astype(jnp.float32)
    total = jnp.concatenate([total_own, total_other], axis=0).astype(bf16)
    back = ((states[:, None] == order_cat[None, :]) & live_out[:, None]).astype(bf16)
    return dot(back, total).astype(bf16)[None]


def solution(mesh):
    in_specs = (
        P("chan", "row", "col"),
        P("chan", "col", "row"),
        P("chan", "col", "row"),
        P(None, "chan"),
        P("chan", None),
        P("chan"),
    )
    out_specs = P("chan", "col", "row")
    sizes = mesh.shape
    paired = sizes["chan"] == 2 and sizes["row"] == 4 and sizes["col"] == 4

    def update(*args):
        single = args[3].shape[0] == sizes["chan"]
        body = pair_shards if paired and single else general_shards
        return jax.shard_map(
            body, mesh=mesh, in_specs=in_specs, out_specs=out_specs, check_vma=False
        )(*args)

    return update
```
